128 devices in a mesh: cuts: 2 (over x_hi), section: 4 (over y), dp: 16 (over z, x_lo, core).
Axes of the slice: x: 4 (x_hi: 2, x_lo: 2; x = x_hi * 2 + x_lo), y: 4, z: 4, core: 2. Of those that a mesh axis runs over, the one named last changes fastest.
Arguments:
- activations: bfloat16 [2, 4, 4096, 4096], P('cuts', 'section', 'dp'), may hold values from -6 to 6
- upstream_grad: bfloat16 [2, 4, 4096, 4096], P('cuts', 'section', 'dp'), may hold values from -6 to 6
- routes: int32 [2, 4, 4096, 4], P('cuts', 'section', 'dp'), may hold values from 0 to 15, as said below
- router_probs: float32 [2, 4, 4096, 4], P('cuts', 'section', 'dp'), may hold values from 0.2 to 1
- gate_weight: bfloat16 [4, 5376, 4096], P('section', 'dp'), may hold values from -0.09375 to 0.09375
- up_weight: bfloat16 [4, 5376, 4096], P('section', 'dp'), may hold values from -0.09375 to 0.09375
- down_weight: bfloat16 [4, 5376, 4096], P('section', 'dp'), may hold values from -0.078125 to 0.078125
Outputs:
- grad_gate: bfloat16 [4, 5376, 4096], P('section', 'dp')
- grad_up: bfloat16 [4, 5376, 4096], P('section', 'dp')
- grad_down: bfloat16 [4, 5376, 4096], P('section', 'dp')
- prev_grad: bfloat16 [2, 4, 4096, 4096], P('cuts', 'section', 'dp')
The draws below stay inside these ranges and needn't reach their ends.
Inputs may be any that keep to these rules, and one draw needn't show every extreme that they name: `routes`: each token names 4 different experts. In every aligned block of 256 tokens of one replica and section, from 32 to 64 tokens name expert 0, and in every draw some block has exactly 64.
All inputs are finite; a program needn't handle non-finite values.
Results may differ from the reference program's by a relative error of at most 0.025.
Values may be sent and summed in bfloat16 or wider, within the bound.
No kernel may reach another device: no remote copies, remote signals or barrier semaphores. Data moves between devices by JAX's collectives and lax.ppermute only.
A program may use at most 192 MiB of HBM per device.

```python
import jax
import jax.numpy as jnp
from jax import lax

D = 4096
FFW = 5376
EXPERTS = 16
TOP = 4
TOK_DEV = 256
CAP = 64
ROWS = 1024
TOKENS = 4096
N_CUTS = 2
N_SECTION = 4
N_DP = 16


def draw_routes(key, part):
    blocks = N_CUTS * N_SECTION * N_DP
    key_count, key_full, key_rank, key_other, key_place = jax.random.split(key, 5)
    counts = jax.random.randint(key_count, (blocks,), CAP // 2, CAP + 1)
    fullest = jax.random.randint(key_full, (), 0, blocks)
    counts = jnp.where(jnp.arange(blocks) == fullest, CAP, counts)
    ranking = jax.vmap(lambda one_key: jax.random.permutation(one_key, TOK_DEV))(jax.random.split(key_rank, blocks))
    chosen = (ranking < counts[:, None]).reshape(-1)
    others = jax.vmap(lambda one_key: jax.random.permutation(one_key, EXPERTS - 1) + 1)(jax.random.split(key_other, blocks * TOK_DEV))
    others = others[:, :TOP]
    position = jax.random.randint(key_place, (blocks * TOK_DEV,), 0, TOP)
    put_zero = chosen[:, None] & (jnp.arange(TOP)[None, :] == position[:, None])
    expert_ids = jnp.where(put_zero, 0, others)
    return expert_ids.reshape(N_CUTS, N_SECTION, TOKENS, TOP).astype(jnp.int32)


def block_levels(own_key, shape, cuts, smallest, high):
    factor_of, own = 1.0, jax.random.fold_in(own_key, 6)
    for dim, blocks in cuts:
        draws = jnp.exp(jax.random.uniform(jax.random.fold_in(own, dim), (blocks,), jnp.float32, smallest / len(cuts), high / len(cuts)))
        factor_of = factor_of * jnp.repeat(draws, shape[dim] // blocks).reshape([-1 if axis == dim else 1 for axis in range(len(shape))])
    return factor_of


def scatter_about(rng, extent, width, most, shards=(), kind=jnp.bfloat16):
    values = jax.random.normal(rng, extent, jnp.float32) * width
    if len(shards) > 0:
        values = block_levels(rng, extent, shards, -0.22, 0.18) * values
    return jnp.clip(values, min=-most, max=most).astype(kind)


def setup_inputs(seed: int = 0) -> dict:
    keys = jax.random.split(jax.random.key(seed), 8)
    activations = scatter_about(keys[0], (N_CUTS, N_SECTION, TOKENS, D), 1.0, 6.0, ((0, 2), (1, 4), (2, 16)))
    upstream_grad = scatter_about(keys[1], (N_CUTS, N_SECTION, TOKENS, D), 1.0, 6.0, ((0, 2), (1, 4), (2, 16)))
    routes = draw_routes(jax.random.fold_in(keys[7], 71), 0)
    router_probs = jnp.clip(0.2 + 0.8 * jax.random.uniform(keys[3], (N_CUTS, N_SECTION, TOKENS, TOP), jnp.float32) ** block_levels(keys[3], (N_CUTS, N_SECTION, TOKENS, TOP), ((0, 2), (1, 4), (2, 16)), -0.2, 0.2), 0.2, 1.0)
    gate_weight = scatter_about(keys[4], (N_SECTION, FFW, D), D ** -0.5, 0.09375, ((0, 4), (1, 16)))
    up_weight = scatter_about(keys[5], (N_SECTION, FFW, D), D ** -0.5, 0.09375, ((0, 4), (1, 16)))
    down_weight = scatter_about(keys[6], (N_SECTION, FFW, D), FFW ** -0.5, 0.078125, ((0, 4), (1, 16)))
    return dict(activations=activations, upstream_grad=upstream_grad, routes=routes, router_probs=router_probs, gate_weight=gate_weight, up_weight=up_weight, down_weight=down_weight)


def make_picker(is_routed):
    blocks_routed = is_routed.reshape(N_DP, TOK_DEV)
    row_index = jnp.cumsum(blocks_routed.astype(jnp.int32), axis=1) - 1
    wanted = jnp.arange(CAP, dtype=jnp.int32)
    picker = (row_index[:, None, :] == wanted[None, :, None]) & blocks_routed[:, None, :]
    return picker.astype(jnp.float32)


def pick_rows(picker, values):
    blocks = values.astype(jnp.float32).reshape(N_DP, TOK_DEV, D)
    packed = jnp.einsum("nct,ntd->ncd", picker, blocks)
    return packed.reshape(ROWS, D).astype(jnp.bfloat16)


def slice_backward(activations, upstream, routes, probs, gate_w, up_w, down_w):
    expert_hits = routes == 0
    router_weight = jnp.sum(jnp.where(expert_hits, probs, jnp.float32(0.0)), axis=1)
    is_routed = jnp.any(expert_hits, axis=1)
    scaled = (router_weight[:, None] * upstream.astype(jnp.float32)).astype(jnp.bfloat16)
    picker = make_picker(is_routed)
    rows_acts = pick_rows(picker, activations)
    rows_grads = pick_rows(picker, scaled)
    gate_pre = jnp.dot(rows_acts, gate_w.T, preferred_element_type=jnp.float32)
    up_pre = jnp.dot(rows_acts, up_w.T, preferred_element_type=jnp.float32)
    sig_gate = jax.nn.sigmoid(gate_pre)
    silu_gate = gate_pre * sig_gate
    hidden = (silu_gate * up_pre).astype(jnp.bfloat16)
    hidden_grad = jnp.dot(rows_grads, down_w.T, preferred_element_type=jnp.float32)
    gate_grad = (hidden_grad * up_pre * sig_gate * (1.0 + gate_pre * (1.0 - sig_gate))).astype(jnp.bfloat16)
    up_grad = (hidden_grad * silu_gate).astype(jnp.bfloat16)
    down_part = jnp.dot(hidden.T, rows_grads, preferred_element_type=jnp.float32)
    gate_part = jnp.dot(gate_grad.T, rows_acts, preferred_element_type=jnp.float32)
    up_part = jnp.dot(up_grad.T, rows_acts, preferred_element_type=jnp.float32)
    hid_dev = FFW // N_DP
    gate_blocks = gate_grad.astype(jnp.float32).reshape(ROWS, N_DP, hid_dev)
    up_blocks = up_grad.astype(jnp.float32).reshape(ROWS, N_DP, hid_dev)
    gate_wblocks = gate_w.astype(jnp.float32).reshape(N_DP, hid_dev, D)
    up_wblocks = up_w.astype(jnp.float32).reshape(N_DP, hid_dev, D)
    terms = jnp.einsum("rnh,nhd->nrd", gate_blocks, gate_wblocks) + jnp.einsum("rnh,nhd->nrd", up_blocks, up_wblocks)
    terms = lax.optimization_barrier(terms.astype(jnp.bfloat16)).astype(jnp.float32)
    input_rows = jnp.sum(terms, axis=0).astype(jnp.bfloat16)
    back = jnp.einsum("nct,ncd->ntd", picker, input_rows.astype(jnp.float32).reshape(N_DP, CAP, D))
    token_grad = back.reshape(TOKENS, D).astype(jnp.bfloat16)
    return gate_part, up_part, down_part, token_grad


def reference(activations, upstream_grad, routes, router_probs, gate_weight, up_weight, down_weight):
    gate_out = []
    up_out = []
    down_out = []
    token_grads = [[None] * N_SECTION for replica in range(N_CUTS)]
    for section_id in range(N_SECTION):
        gate_total = jnp.zeros((FFW, D), jnp.float32)
        up_total = jnp.zeros((FFW, D), jnp.float32)
        down_total = jnp.zeros((FFW, D), jnp.float32)
        for replica in range(N_CUTS):
            gate_part, up_part, down_part, token_grad = slice_backward(
                activations[replica, section_id], upstream_grad[replica, section_id],
                routes[replica, section_id], router_probs[replica, section_id],
                gate_weight[section_id], up_weight[section_id], down_weight[section_id])
            parts = lax.optimization_barrier((gate_part.astype(jnp.bfloat16), up_part.astype(jnp.bfloat16), down_part.astype(jnp.bfloat16)))
            gate_total = gate_total + parts[0].astype(jnp.float32)
            up_total = up_total + parts[1].astype(jnp.float32)
            down_total = down_total + parts[2].astype(jnp.float32)
            token_grads[replica][section_id] = token_grad
        gate_out.append(gate_total.astype(jnp.bfloat16))
        up_out.append(up_total.astype(jnp.bfloat16))
        down_out.append(down_total.astype(jnp.bfloat16))
    zero_rows = jnp.zeros((TOKENS, D), jnp.bfloat16)
    received = []
    for replica in range(N_CUTS):
        row_list = []
        for section_id in range(N_SECTION):
            if section_id + 1 < N_SECTION:
                row_list.append(token_grads[replica][section_id + 1])
            else:
                row_list.append(zero_rows)
        received.append(jnp.stack(row_list, axis=0))
    prev_grad = jnp.stack(received, axis=0)
    return jnp.stack(gate_out, axis=0), jnp.stack(up_out, axis=0), jnp.stack(down_out, axis=0), prev_grad
```

```python
import jax
import jax.numpy as jnp
from jax import lax
from jax.sharding import PartitionSpec as P

CAP = 64
AXES = ("cuts", "dp")


def place(x, z, core):
    return (x // 2) * 16 + z * 4 + (x % 2) * 2 + core


def route(fx, fz, fc):
    return [
        (place(x, z, c), place(fx(x) % 4, fz(z) % 4, fc(c)))
        for x in range(4)
        for z in range(4)
        for c in range(2)
    ]


def keep(v):
    return v


INNER = route(lambda x: x ^ 1, keep, keep)
OUTER = route(lambda x: 3 - x, keep, keep)
UP = route(keep, lambda z: z + 1, keep)
DOWN = route(keep, lambda z: z - 1, keep)
ACROSS = route(keep, lambda z: z + 2, keep)
SIBLING = route(keep, keep, lambda c: 1 - c)


def send(value, pairs):
    return lax.ppermute(value, AXES, pairs)


def join(*parts):
    return jnp.concatenate(parts, axis=0)


def x_ring(v):
    h = v.shape[0] // 2
    inner, outer = send(v, INNER), send(v, OUTER)
    return inner, outer, send(outer[:h], INNER), send(inner[h:], OUTER)


def z_ring(v):
    h = v.shape[0] // 2
    below, above = send(v, UP), send(v, DOWN)
    return below, above, send(below[:h], UP), send(above[h:], DOWN)


def contract_last(left, right):
    return lax.dot_general(
        left, right, (((1,), (1,)), ((), ())), preferred_element_type=jnp.float32
    )


def contract_first(left, right):
    return lax.dot_general(
        left, right, (((0,), (0,)), ((), ())), preferred_element_type=jnp.float32
    )


def matmul(left, right):
    return jnp.dot(left, right, preferred_element_type=jnp.float32)


def half(v):
    return v.astype(jnp.bfloat16)


def full(v):
    return v.astype(jnp.float32)


def per_device(
    activations, upstream_grad, routes, router_probs, gate_weight, up_weight, down_weight
):
    local_acts = activations[0, 0]
    local_grads = upstream_grad[0, 0]
    expert_hits = routes[0, 0] == 0
    router_weight = jnp.sum(jnp.where(expert_hits, router_probs[0, 0], jnp.float32(0.0)), axis=1)
    is_routed = jnp.any(expert_hits, axis=1)
    before = jnp.arange(256)[None, :] <= jnp.arange(256)[:, None]
    count = jnp.sum(jnp.where(before & is_routed[None, :], 1, 0), axis=1)
    slot = jnp.where(is_routed, count, 0)
    wanted = jnp.arange(1, CAP + 1, dtype=jnp.int32)
    picker = half(slot[None, :] == wanted[:, None])
    scaled = half(router_weight[:, None] * full(local_grads))
    acts = half(matmul(picker, local_acts))
    grads = half(matmul(picker, scaled))
    next_slot = lax.ppermute(slot, "section", [(1, 0), (2, 1), (3, 2)])
    gate_local, up_local, down_local = gate_weight[0], up_weight[0], down_weight[0]

    acts_x = join(acts, *x_ring(acts))
    grads_z = join(grads, *z_ring(grads))
    near, far = acts_x[:128], acts_x[128:]
    near_z = z_ring(near)
    far_z = z_ring(far)
    grads_x = x_ring(grads_z)
    def column(base, ring, k):
        across = join(ring[2], ring[3])
        return join(*[v[k * 64 : k * 64 + 64] for v in (base, ring[0], ring[1], across)])

    acts_of = [column(near, near_z, 0), column(near, near_z, 1), column(far, far_z, 0), column(far, far_z, 1)]
    grads_of = [grads_z, grads_x[0], grads_x[1], join(grads_x[2], grads_x[3])]

    def forward(rows_acts, rows_grads):
        gate_pre = contract_last(rows_acts, gate_local)
        up_pre = contract_last(rows_acts, up_local)
        sig_gate = jax.nn.sigmoid(gate_pre)
        silu_gate = gate_pre * sig_gate
        hidden_grad = contract_last(rows_grads, down_local)
        hidden = half(silu_gate * up_pre)
        gate_grad = half(hidden_grad * up_pre * sig_gate * (1.0 + gate_pre * (1.0 - sig_gate)))
        up_grad = half(hidden_grad * silu_gate)
        return hidden, gate_grad, up_grad

    all_acts, all_grads, outs = [], [], []
    for k in range(4):
        mine = join(acts_of[k], grads_of[k])
        theirs = send(mine, SIBLING)
        rows_a = join(mine[:256], theirs[:256])
        rows_g = join(mine[256:], theirs[256:])
        all_acts.append(rows_a)
        all_grads.append(rows_g)
        outs.append(forward(rows_a, rows_g))

    terms = [half(matmul(outs[k][1], gate_local) + matmul(outs[k][2], up_local)) for k in range(2)]
    from_core = send(join(terms[0][256:], terms[1][256:]), SIBLING)
    own = half(full(terms[0][:256]) + full(from_core[:256]))
    inner = half(full(terms[1][:256]) + full(from_core[256:]))
    own_l, inner_l, own_r, inner_r = own[:, :2048], inner[:, :2048], own[:, 2048:], inner[:, 2048:]
    both_r = join(own_r.reshape(4, 64, 2048), inner_r.reshape(4, 64, 2048)).reshape(2, 4, 64, 2048)
    left = full(own_l) + full(send(inner_l, INNER))
    z_r = [
        full(both_r[:, 0]),
        full(send(both_r[:, 1], DOWN)),
        full(send(both_r[:, 2], UP)),
        full(send(both_r[:, 3], ACROSS)),
    ]
    right2 = (z_r[0] + z_r[1]) + (z_r[2] + z_r[3])
    right = right2[0] + full(send(half(right2[1]), INNER))
    left_b = half(left)
    left = (left[:64] + full(send(left_b[64:128], DOWN))) + (
        full(send(left_b[128:192], UP)) + full(send(left_b[192:], ACROSS))
    )
    input_rows = jnp.concatenate([half(left), half(right)], axis=1)
    shifted = lax.ppermute(input_rows, "section", [(1, 0), (2, 1), (3, 2)])
    placer = half(next_slot[:, None] == wanted[None, :])
    prev_grad = half(matmul(placer, shifted))[None, None]

    rows_acts, rows_grads = join(*all_acts), join(*all_grads)
    hidden, gate_grad, up_grad = (join(*[o[i] for o in outs]) for i in range(3))
    grad_down = half(contract_first(hidden, rows_grads))[None]
    grad_gate = half(contract_first(gate_grad, rows_acts))[None]
    grad_up = half(contract_first(up_grad, rows_acts))[None]
    return (grad_gate, grad_up, grad_down, prev_grad)


def solution(mesh):
    placed = (
        P("cuts", "section", "dp", None),
        P("cuts", "section", "dp", None),
        P("cuts", "section", "dp", None),
        P("cuts", "section", "dp", None),
        P("section", "dp", None),
        P("section", "dp", None),
        P("section", "dp", None),
    )
    return jax.shard_map(
        per_device,
        mesh=mesh,
        in_specs=placed,
        out_specs=(
            P("section", "dp", None),
            P("section", "dp", None),
            P("section", "dp", None),
            P("cuts", "section", "dp", None),
        ),
        check_vma=False,
    )
```

```python
import jax
import jax.numpy as jnp
from jax import lax
from jax.experimental import pallas as pl
from jax.experimental.pallas import tpu as pltpu
from jax.sharding import PartitionSpec as P

CAP = 64
AXES = ("cuts", "dp")


def place(x, z, core):
    return (x // 2) * 16 + z * 4 + (x % 2) * 2 + core


def route(fx, fz, fc):
    return [
        (place(x, z, c), place(fx(x) % 4, fz(z) % 4, fc(c)))
        for x in range(4)
        for z in range(4)
        for c in range(2)
    ]


def keep(v):
    return v


INNER = route(lambda x: x ^ 1, keep, keep)
OUTER = route(lambda x: 3 - x, keep, keep)
UP = route(keep, lambda z: z + 1, keep)
DOWN = route(keep, lambda z: z - 1, keep)
ACROSS = route(keep, lambda z: z + 2, keep)
SIBLING = route(keep, keep, lambda c: 1 - c)


def send(value, pairs):
    return lax.ppermute(value, AXES, pairs)


def join(*parts):
    return jnp.concatenate(parts, axis=0)


def contract_last(left, right):
    return lax.dot_general(
        left, right, (((1,), (1,)), ((), ())), preferred_element_type=jnp.float32
    )


def contract_first(left, right):
    return lax.dot_general(
        left, right, (((0,), (0,)), ((), ())), preferred_element_type=jnp.float32
    )


def matmul(left, right):
    return jnp.dot(left, right, preferred_element_type=jnp.float32)


def half(v):
    return v.astype(jnp.bfloat16)


def full(v):
    return v.astype(jnp.float32)


def weight_grads(pairs, outs):
    tile = 256
    n = len(pairs)

    def kernel(*refs):
        pair_refs, out_refs, results = refs[:n], refs[n : 4 * n], refs[4 * n :]
        for which in range(3):
            total = None
            for k in range(n):
                rows = pairs[k].shape[0] // 2
                right = pair_refs[k][rows:, :] if which == 0 else pair_refs[k][:rows, :]
                part = matmul(out_refs[3 * k + which][...], right)
                total = part if total is None else total + part
            results[which][...] = total.astype(jnp.bfloat16)

    flat = [o for out in outs for o in out]
    units, width = flat[0].shape[0], pairs[0].shape[1]
    return pl.pallas_call(
        kernel,
        grid=(width // tile,),
        in_specs=[pl.BlockSpec((p.shape[0], tile), lambda j: (0, j)) for p in pairs]
        + [pl.BlockSpec(o.shape, lambda j: (0, 0), pipeline_mode=pl.Buffered(1)) for o in flat],
        out_specs=[pl.BlockSpec((units, tile), lambda j: (0, j))] * 3,
        out_shape=[jax.ShapeDtypeStruct((units, width), jnp.bfloat16)] * 3,
        compiler_params=pltpu.CompilerParams(vmem_limit_bytes=40 << 20),
        cost_estimate=pl.CostEstimate(
            flops=6 * 2048 * units * width, bytes_accessed=4 * 2048 * width + 6 * units * width, transcendentals=0
        ),
    )(*pairs, *flat)


def together(*values):
    return lax.optimization_barrier(values)


def per_device(
    activations, upstream_grad, routes, router_probs, gate_weight, up_weight, down_weight
):
    local_acts = activations[0, 0]
    local_grads = upstream_grad[0, 0]
    expert_hits = routes[0, 0] == 0
    router_weight = jnp.sum(jnp.where(expert_hits, router_probs[0, 0], jnp.float32(0.0)), axis=1)
    is_routed = jnp.any(expert_hits, axis=1)
    before = jnp.arange(256)[None, :] <= jnp.arange(256)[:, None]
    count = jnp.sum(jnp.where(before & is_routed[None, :], 1, 0), axis=1)
    slot = jnp.where(is_routed, count, 0)
    wanted = jnp.arange(1, CAP + 1, dtype=jnp.int32)
    picker = half(slot[None, :] == wanted[:, None])
    scaled = half(router_weight[:, None] * full(local_grads))
    a = half(matmul(picker, local_acts))
    g = half(matmul(picker, scaled))
    gate_local, up_local, down_local = gate_weight[0], up_weight[0], down_weight[0]

    def forward(pair):
        rows = pair.shape[0] // 2
        rows_acts, rows_grads = pair[:rows], pair[rows:]
        gate_pre = contract_last(gate_local, rows_acts)
        up_pre = contract_last(up_local, rows_acts)
        sig_gate = jax.nn.sigmoid(gate_pre)
        silu_gate = gate_pre * sig_gate
        hidden_grad = contract_last(down_local, rows_grads)
        hidden = half(silu_gate * up_pre)
        gate_grad = half(hidden_grad * up_pre * sig_gate * (1.0 + gate_pre * (1.0 - sig_gate)))
        up_grad = half(hidden_grad * silu_gate)
        return hidden, gate_grad, up_grad

    def input_term(out):
        return contract_first(out[1], gate_local) + contract_first(out[2], up_local)

    a, g = together(a, g)
    a_is, a_os, g_sb, g_su = send(a, INNER), send(a, OUTER), send(g, UP), send(g, DOWN)
    to_i, to_o, to_u, to_b, slot_out, a, g = together(
        join(a_os[:32], g, g_sb, g_su),
        join(a_is[32:], g, g_sb, g_su),
        join(g_sb[:32], a, a_is, a_os),
        join(g_su[32:], a, a_is, a_os),
        slot,
        a,
        g,
    )
    from_i, from_o, from_b, from_u = send(to_i, INNER), send(to_o, OUTER), send(to_u, UP), send(to_b, DOWN)
    next_slot = lax.ppermute(slot_out, "section", [(1, 0), (2, 1), (3, 2)])
    own_pair = join(
        a, a_is, from_b[32:160], from_u[32:160],
        g, from_i[32:96], g_sb, from_i[96:160], g_su, from_i[160:224],
    )
    a_ts, g_st = join(from_i[:32], from_o[:32]), join(from_b[:32], from_u[:32])
    own_pair, g_st, a_sb, a_iu, next_slot, from_i, from_o, from_b, from_u = together(
        own_pair, g_st, from_b[32:96], from_u[96:160], next_slot, from_i, from_o, from_b, from_u
    )
    g_it, g_ot, a_st, a_it = send(g_st, INNER), send(g_st, OUTER), send(a_sb, UP), send(a_iu, DOWN)
    own_other = send(own_pair, SIBLING)
    far_pair = join(a_st, a_it, g_st, g_it)
    to_i, to_o, to_u, to_b, a_ts, far_pair, own_pair, own_other, g_ot = together(
        from_o[32:160],
        join(from_i[160:224], g_it),
        join(a_ts, from_b[160:192]),
        join(a_ts, from_u[192:224]),
        a_ts,
        far_pair,
        own_pair,
        own_other,
        g_ot,
    )
    far_other = send(far_pair, SIBLING)
    g_t1, g_t2, a_tb, a_tu = send(to_i, INNER), send(to_o, OUTER), send(to_u, UP), send(to_b, DOWN)
    a_tt = send(a_ts, ACROSS)
    out_own, out_own2 = forward(own_pair), forward(own_other)
    term_own, term_own2 = input_term(out_own), half(input_term(out_own2))
    term_from = send(term_own2, SIBLING)
    out_far, out_far2 = forward(far_pair), forward(far_other)
    term_far, term_far2 = input_term(out_far), half(input_term(out_far2))
    far_from = send(term_far2, SIBLING)
    own = half(term_own + full(term_from))
    far = half(term_far + full(far_from))
    x1_pair = join(a_os, from_b[160:224], from_u[160:224], from_o[32:224])
    x2_pair = join(
        a_tb[64:96], a_tu[64:96], a_ts, a_tb[:64], a_tu[:64], a_tt,
        g_ot, g_t1, g_t2,
    )
    to_b, to_u, to_i, own0, far0, x1_pair, x2_pair = together(
        own[128:256], own[256:384], far[64:128], own[:128], far[:64], x1_pair, x2_pair
    )
    z_u, z_b, far_i = send(to_b, DOWN), send(to_u, UP), send(to_i, INNER)
    x1_other, x2_other = send(x1_pair, SIBLING), send(x2_pair, SIBLING)
    out_x1, out_x2 = forward(x1_pair), forward(x2_pair)
    out_x12, out_x22 = forward(x1_other), forward(x2_other)
    near = full(own0) + full(z_u) + full(z_b)
    to_i, to_t, near_s, done_x = together(
        half(near[64:]), half(full(far0) + full(far_i)), near[:64], (out_x1, out_x2, out_x12, out_x22)
    )
    out_x1, out_x2, out_x12, out_x22 = done_x
    near_i, far_t = send(to_i, INNER), send(to_t, ACROSS)
    input_rows = half(near_s + full(near_i) + full(far_t))
    shifted = lax.ppermute(input_rows, "section", [(1, 0), (2, 1), (3, 2)])
    placer = half(next_slot[:, None] == wanted[None, :])
    prev_grad = half(matmul(placer, shifted))[None, None]

    pairs = [own_pair, own_other, far_pair, far_other, x1_pair, x1_other, x2_pair, x2_other]
    outs = [out_own, out_own2, out_far, out_far2, out_x1, out_x12, out_x2, out_x22]
    grad_down, grad_gate, grad_up = weight_grads(pairs, outs)
    return (grad_gate[None], grad_up[None], grad_down[None], prev_grad)


def solution(mesh):
    placed = (
        P("cuts", "section", "dp", None),
        P("cuts", "section", "dp", None),
        P("cuts", "section", "dp", None),
        P("cuts", "section", "dp", None),
        P("section", "dp", None),
        P("section", "dp", None),
        P("section", "dp", None),
    )
    return jax.shard_map(
        per_device,
        mesh=mesh,
        in_specs=placed,
        out_specs=(
            P("section", "dp", None),
            P("section", "dp", None),
            P("section", "dp", None),
            P("cuts", "section", "dp", None),
        ),
        check_vma=False,
    )
```

```python
import jax
import jax.numpy as jnp
from jax import lax
from jax.experimental import pallas as pl
from jax.experimental.pallas import tpu as pltpu
from jax.sharding import PartitionSpec as P

CAP = 64
AXES = ("cuts", "dp")


def place(x, z, core):
    return (x // 2) * 16 + z * 4 + (x % 2) * 2 + core


def route(fx, fz, fc):
    return [
        (place(x, z, c), place(fx(x) % 4, fz(z) % 4, fc(c)))
        for x in range(4)
        for z in range(4)
        for c in range(2)
    ]


def keep(v):
    return v


INNER = route(lambda x: x ^ 1, keep, keep)
OUTER = route(lambda x: 3 - x, keep, keep)
UP = route(keep, lambda z: z + 1, keep)
DOWN = route(keep, lambda z: z - 1, keep)
ACROSS = route(keep, lambda z: z + 2, keep)
SIBLING = route(keep, keep, lambda c: 1 - c)


def send(value, pairs):
    return lax.ppermute(value, AXES, pairs)


def join(*parts):
    return jnp.concatenate(parts, axis=0)


def contract_last(left, right):
    return lax.dot_general(
        left, right, (((1,), (1,)), ((), ())), preferred_element_type=jnp.float32
    )


def contract_first(left, right):
    return lax.dot_general(
        left, right, (((0,), (0,)), ((), ())), preferred_element_type=jnp.float32
    )


def matmul(left, right):
    return jnp.dot(left, right, preferred_element_type=jnp.float32)


def half(v):
    return v.astype(jnp.bfloat16)


def full(v):
    return v.astype(jnp.float32)


SMALL = pl.CostEstimate(flops=1 << 36, bytes_accessed=1 << 30, transcendentals=0)
GAP = 384
FWD, TERM, SUMS = 14, 10, 24
ON_CHIP = pl.BlockSpec(memory_space=pltpu.VMEM)


def forward(pair, other, gate, up, down):
    tile = 1024
    m, (units, width) = pair.shape[0] // 2, gate.shape

    def kernel(pair_ref, other_ref, gate_ref, up_ref, down_ref, hidden_ref, grads_ref, acc):
        acc[...] = jnp.zeros_like(acc)

        @pl.loop(0, width // tile)
        def _(step):
            at = pl.ds(pl.multiple_of(step * tile, tile), tile)
            rows_acts = join(pair_ref[:m, at], other_ref[:m, at])
            rows_grads = join(pair_ref[m:, at], other_ref[m:, at])
            acc[0] += contract_last(gate_ref[:, at], rows_acts)
            acc[1] += contract_last(up_ref[:, at], rows_acts)
            acc[2] += contract_last(down_ref[:, at], rows_grads)

        gate_pre, up_pre, hidden_grad = acc[0], acc[1], acc[2]
        sig_gate = jax.nn.sigmoid(gate_pre)
        silu_gate = gate_pre * sig_gate
        hidden_ref[...] = half(silu_gate * up_pre)
        grads_ref[:units, :] = half(
            hidden_grad * up_pre * sig_gate * (1.0 + gate_pre * (1.0 - sig_gate))
        )
        grads_ref[GAP : GAP + units, :] = half(hidden_grad * silu_gate)
        blank = jnp.zeros((GAP - units, 2 * m), jnp.bfloat16)
        grads_ref[units:GAP, :] = blank
        grads_ref[GAP + units :, :] = blank

    return pl.pallas_call(
        kernel,
        in_specs=[ON_CHIP] * 5,
        out_specs=[ON_CHIP] * 2,
        out_shape=[
            jax.ShapeDtypeStruct((units, 2 * m), jnp.bfloat16),
            jax.ShapeDtypeStruct((2 * GAP, 2 * m), jnp.bfloat16),
        ],
        scratch_shapes=[pltpu.VMEM((3, units, 2 * m), jnp.float32)],
        compiler_params=pltpu.CompilerParams(vmem_limit_bytes=FWD << 20),
        cost_estimate=SMALL,
    )(pair, other, gate, up, down)


def input_terms(grads, gate, up):
    tile = 512
    n, (units, width) = grads.shape[1], gate.shape
    m = n // 2

    def kernel(grads_ref, gate_ref, up_ref, own_ref, other_ref, left, right):
        left[...] = grads_ref[...].T
        right[...] = jnp.zeros_like(right)

        @pl.loop(0, width // tile)
        def _(step):
            at = pl.ds(pl.multiple_of(step * tile, tile), tile)
            right[:units, :] = gate_ref[:, at]
            right[GAP : GAP + units, :] = up_ref[:, at]
            term = half(matmul(left[...], right[...]))
            own_ref[:, at] = term[:m]
            other_ref[:, at] = term[m:]

    return pl.pallas_call(
        kernel,
        in_specs=[ON_CHIP] * 3,
        out_specs=[ON_CHIP] * 2,
        out_shape=[jax.ShapeDtypeStruct((m, width), jnp.bfloat16)] * 2,
        scratch_shapes=[
            pltpu.VMEM((n, 2 * GAP), jnp.bfloat16),
            pltpu.VMEM((2 * GAP, tile), jnp.bfloat16),
        ],
        compiler_params=pltpu.CompilerParams(vmem_limit_bytes=TERM << 20),
        cost_estimate=SMALL,
    )(grads, gate, up)


def weight_grads(pairs, hiddens, grads, first, count, earlier):
    tile = 512
    n = len(pairs)
    units, width = hiddens[0].shape[0], pairs[0].shape[1]
    total = sum(p.shape[0] for p in pairs) // 2
    kept = len(earlier)

    def kernel(*refs):
        pair_refs, hidden_refs, grads_refs = refs[:n], refs[n : n + n // 2], refs[n + n // 2 : 2 * n]
        gate_out, up_out, down_out = refs[2 * n + kept : 2 * n + kept + 3]
        acts, rows_grads, hidden, grad, sems = refs[2 * n + kept + 3 :]
        step = pl.program_id(0)

        def copies(at, slot):
            columns = pl.ds(pl.multiple_of((first + at) * tile, tile), tile)
            made, start = [], 0
            for k in range(n):
                m = pairs[k].shape[0] // 2
                for part, dst in ((0, acts), (1, rows_grads)):
                    made.append(
                        pltpu.make_async_copy(
                            pair_refs[k].at[pl.ds(part * m, m), columns],
                            dst.at[slot, pl.ds(start, m), :],
                            sems.at[slot, 2 * k + part],
                        )
                    )
                start += m
            return made

        @pl.when(step == 0)
        def _():
            for c in copies(0, 0):
                c.start()
            start = 0
            for k in range(n // 2):
                m = hidden_refs[k].shape[1]
                hidden[:, start : start + m] = hidden_refs[k][...]
                grad[:, start : start + m] = grads_refs[k][...]
                start += m

        slot = lax.rem(step, 2)

        @pl.when(step + 1 < count)
        def _():
            for c in copies(step + 1, 1 - slot):
                c.start()

        for c in copies(step, slot):
            c.wait()
        right = acts[slot]
        gate_out[...] = half(matmul(grad[:units, :], right))
        up_out[...] = half(matmul(grad[GAP : GAP + units, :], right))
        down_out[...] = half(matmul(hidden[...], rows_grads[slot]))

    whole = [
        pl.BlockSpec(v.shape, lambda j: (0, 0), pipeline_mode=pl.Buffered(1)) for v in hiddens + grads
    ]
    hbm = pl.BlockSpec(memory_space=pl.ANY)
    return pl.pallas_call(
        kernel,
        grid=(count,),
        in_specs=[hbm] * n + whole + [hbm] * kept,
        out_specs=[pl.BlockSpec((units, tile), lambda j: (0, first + j))] * 3,
        out_shape=[jax.ShapeDtypeStruct((units, width), jnp.bfloat16)] * 3,
        input_output_aliases={2 * n + i: i for i in range(kept)},
        scratch_shapes=[
            pltpu.VMEM((2, total, tile), jnp.bfloat16),
            pltpu.VMEM((2, total, tile), jnp.bfloat16),
            pltpu.VMEM((units, total), jnp.bfloat16),
            pltpu.VMEM((2 * GAP, total), jnp.bfloat16),
            pltpu.SemaphoreType.DMA((2, 2 * n)),
        ],
        compiler_params=pltpu.CompilerParams(vmem_limit_bytes=SUMS << 20),
        cost_estimate=SMALL,
    )(*pairs, *hiddens, *grads, *earlier)


def together(*values):
    return lax.optimization_barrier(values)


def per_device(
    activations, upstream_grad, routes, router_probs, gate_weight, up_weight, down_weight
):
    local_acts = activations[0, 0]
    local_grads = upstream_grad[0, 0]
    expert_hits = routes[0, 0] == 0
    router_weight = jnp.sum(jnp.where(expert_hits, router_probs[0, 0], jnp.float32(0.0)), axis=1)
    is_routed = jnp.any(expert_hits, axis=1)
    before = jnp.arange(256)[None, :] <= jnp.arange(256)[:, None]
    count = jnp.sum(jnp.where(before & is_routed[None, :], 1, 0), axis=1)
    slot = jnp.where(is_routed, count, 0)
    wanted = jnp.arange(1, CAP + 1, dtype=jnp.int32)
    picker = half(slot[None, :] == wanted[:, None])
    scaled = half(router_weight[:, None] * full(local_grads))
    a = half(matmul(picker, local_acts))
    g = half(matmul(picker, scaled))
    gate_local, up_local, down_local = gate_weight[0], up_weight[0], down_weight[0]

    weights = (gate_local, up_local, down_local)

    a, g = together(a, g)
    a_is, a_os, g_sb, g_su = send(a, INNER), send(a, OUTER), send(g, UP), send(g, DOWN)
    to_i, to_o, to_u, to_b, slot_out, a, g = together(
        join(a_os[:32], g, g_sb, g_su),
        join(a_is[32:], g, g_sb, g_su),
        join(g_sb[:32], a, a_is, a_os),
        join(g_su[32:], a, a_is, a_os),
        slot,
        a,
        g,
    )
    from_i, from_o, from_b, from_u = send(to_i, INNER), send(to_o, OUTER), send(to_u, UP), send(to_b, DOWN)
    next_slot = lax.ppermute(slot_out, "section", [(1, 0), (2, 1), (3, 2)])
    own_pair = join(
        a, a_is, from_b[32:160], from_u[32:160],
        g, from_i[32:96], g_sb, from_i[96:160], g_su, from_i[160:224],
    )
    a_ts, g_st = join(from_i[:32], from_o[:32]), join(from_b[:32], from_u[:32])
    own_pair, g_st, a_sb, a_iu, next_slot, from_i, from_o, from_b, from_u = together(
        own_pair, g_st, from_b[32:96], from_u[96:160], next_slot, from_i, from_o, from_b, from_u
    )
    g_it, g_ot, a_st, a_it = send(g_st, INNER), send(g_st, OUTER), send(a_sb, UP), send(a_iu, DOWN)
    own_other = send(own_pair, SIBLING)
    far_pair = join(a_st, a_it, g_st, g_it)
    to_i, to_o, a_ts, far_pair, own_pair, own_other, g_ot, a_it, from_o, from_b, from_u = together(
        from_o[96:192], join(from_i[192:224], g_it), a_ts, far_pair, own_pair, own_other, g_ot, a_it,
        from_o, from_b, from_u,
    )
    far_other = send(far_pair, SIBLING)
    g_i, g_o, a_tb, a_tu = send(to_i, INNER), send(to_o, OUTER), send(a_ts, UP), send(a_ts, DOWN)
    hidden_far, grads_far = forward(far_pair, far_other, *weights)
    term_far, term_far2 = input_terms(grads_far, gate_local, up_local)
    far_from = send(term_far2, SIBLING)
    hidden_own, grads_own = forward(own_pair, own_other, *weights)
    g_i, g_o, a_tb, a_tu, far_from, grads_own, to_i, to_o, to_u, to_b = together(
        g_i, g_o, a_tb, a_tu, far_from, grads_own, from_o[32:96], a_it, from_b[160:192], from_u[192:224]
    )
    g_ts, a_tt, a_ot1, a_ot2 = send(to_i, INNER), send(to_o, OUTER), send(to_u, UP), send(to_b, DOWN)
    term_own, term_own2 = input_terms(grads_own, gate_local, up_local)
    term_from = send(term_own2, SIBLING)
    far = half(full(term_far) + full(far_from))
    own = half(full(term_own) + full(term_from))
    x1_pair = join(a_os, from_b[160:224], from_u[160:224], from_o[32:224])
    x2_pair = join(a_tb, a_tu, g_i, g_o[:32])
    to_b, to_u, to_i, own0, far0, a_ot1, a_ot2, a_ts, g_ot, g_ts, a_tt, x1_pair, x2_pair = together(
        own[128:256], own[256:384], far[64:128], own[:128], far[:64],
        a_ot1, a_ot2, a_ts, g_ot, g_ts, a_tt, x1_pair, x2_pair,
    )
    z_u, z_b, far_i = send(to_b, DOWN), send(to_u, UP), send(to_i, INNER)
    x3_pair = join(a_ot1, a_ot2, a_ts, a_tt, g_ot, g_ts, g_o[32:])
    x1_other, x2_other, x3_other = send(x1_pair, SIBLING), send(x2_pair, SIBLING), send(x3_pair, SIBLING)
    hidden_x1, grads_x1 = forward(x1_pair, x1_other, *weights)
    hidden_x2, grads_x2 = forward(x2_pair, x2_other, *weights)
    hidden_x3, grads_x3 = forward(x3_pair, x3_other, *weights)
    z_u, z_b, far_i, hidden_x1, hidden_x2, hidden_x3 = together(
        z_u, z_b, far_i, hidden_x1, hidden_x2, hidden_x3
    )
    near = full(own0) + full(z_u) + full(z_b)
    to_i, to_t, near_s = together(half(near[64:]), half(full(far0) + full(far_i)), near[:64])
    near_i, far_t = send(to_i, INNER), send(to_t, ACROSS)
    pairs = [
        own_pair, own_other, far_pair, far_other,
        x1_pair, x1_other, x2_pair, x2_other, x3_pair, x3_other,
    ]
    hiddens = [hidden_own, hidden_far, hidden_x1, hidden_x2, hidden_x3]
    grads = [grads_own, grads_far, grads_x1, grads_x2, grads_x3]
    early = weight_grads(pairs, hiddens, grads, 0, 4, ())
    input_rows, early = together(half(near_s + full(near_i) + full(far_t)), tuple(early))
    shifted = lax.ppermute(input_rows, "section", [(1, 0), (2, 1), (3, 2)])
    placer = half(next_slot[:, None] == wanted[None, :])
    grad_gate, grad_up, grad_down = weight_grads(pairs, hiddens, grads, 4, 4, early)
    prev_grad = half(matmul(placer, shifted))[None, None]
    return (grad_gate[None], grad_up[None], grad_down[None], prev_grad)


def solution(mesh):
    placed = (
        P("cuts", "section", "dp", None),
        P("cuts", "section", "dp", None),
        P("cuts", "section", "dp", None),
        P("cuts", "section", "dp", None),
        P("section", "dp", None),
        P("section", "dp", None),
        P("section", "dp", None),
    )
    return jax.shard_map(
        per_device,
        mesh=mesh,
        in_specs=placed,
        out_specs=(
            P("section", "dp", None),
            P("section", "dp", None),
            P("section", "dp", None),
            P("cuts", "section", "dp", None),
        ),
        check_vma=False,
    )
```

```python
import jax
import jax.numpy as jnp
from jax import lax
from jax.experimental import pallas as pl
from jax.experimental.pallas import tpu as pltpu
from jax.sharding import PartitionSpec as P

CAP = 64
AXES = ("cuts", "dp")


def place(x, z, core):
    return (x // 2) * 16 + z * 4 + (x % 2) * 2 + core


def route(fx, fz, fc):
    return [
        (place(x, z, c), place(fx(x) % 4, fz(z) % 4, fc(c)))
        for x in range(4)
        for z in range(4)
        for c in range(2)
    ]


def keep(v):
    return v


INNER = route(lambda x: x ^ 1, keep, keep)
OUTER = route(lambda x: 3 - x, keep, keep)
UP = route(keep, lambda z: z + 1, keep)
DOWN = route(keep, lambda z: z - 1, keep)
ACROSS = route(keep, lambda z: z + 2, keep)
SIBLING = route(keep, keep, lambda c: 1 - c)


def send(value, pairs):
    return lax.ppermute(value, AXES, pairs)


def join(*parts):
    return jnp.concatenate(parts, axis=0)


def contract_last(left, right):
    return lax.dot_general(
        left, right, (((1,), (1,)), ((), ())), preferred_element_type=jnp.float32
    )


def contract_first(left, right):
    return lax.dot_general(
        left, right, (((0,), (0,)), ((), ())), preferred_element_type=jnp.float32
    )


def matmul(left, right):
    return jnp.dot(left, right, preferred_element_type=jnp.float32)


def half(v):
    return v.astype(jnp.bfloat16)


def full(v):
    return v.astype(jnp.float32)


GAP = 384
FWD, TERM, SUMS = 14, 10, 24
ON_CHIP = pl.BlockSpec(memory_space=pltpu.VMEM)


def cost(effort):
    return pl.CostEstimate(flops=effort, bytes_accessed=1 << 16, transcendentals=0)


def forward(pair, other, gate, up, down, effort):
    tile = 1024
    m, (units, width) = pair.shape[0] // 2, gate.shape

    def kernel(pair_ref, other_ref, gate_ref, up_ref, down_ref, hidden_ref, grads_ref, acc):
        acc[...] = jnp.zeros_like(acc)

        @pl.loop(0, width // tile)
        def _(step):
            at = pl.ds(pl.multiple_of(step * tile, tile), tile)
            rows_acts = join(pair_ref[:m, at], other_ref[:m, at])
            rows_grads = join(pair_ref[m:, at], other_ref[m:, at])
            acc[0] += contract_last(gate_ref[:, at], rows_acts)
            acc[1] += contract_last(up_ref[:, at], rows_acts)
            acc[2] += contract_last(down_ref[:, at], rows_grads)

        gate_pre, up_pre, hidden_grad = acc[0], acc[1], acc[2]
        sig_gate = jax.nn.sigmoid(gate_pre)
        silu_gate = gate_pre * sig_gate
        hidden_ref[...] = half(silu_gate * up_pre)
        grads_ref[:units, :] = half(
            hidden_grad * up_pre * sig_gate * (1.0 + gate_pre * (1.0 - sig_gate))
        )
        grads_ref[GAP : GAP + units, :] = half(hidden_grad * silu_gate)
        blank = jnp.zeros((GAP - units, 2 * m), jnp.bfloat16)
        grads_ref[units:GAP, :] = blank
        grads_ref[GAP + units :, :] = blank

    return pl.pallas_call(
        kernel,
        in_specs=[ON_CHIP] * 5,
        out_specs=[ON_CHIP] * 2,
        out_shape=[
            jax.ShapeDtypeStruct((units, 2 * m), jnp.bfloat16),
            jax.ShapeDtypeStruct((2 * GAP, 2 * m), jnp.bfloat16),
        ],
        scratch_shapes=[pltpu.VMEM((3, units, 2 * m), jnp.float32)],
        compiler_params=pltpu.CompilerParams(vmem_limit_bytes=FWD << 20),
        cost_estimate=cost(effort),
    )(pair, other, gate, up, down)


def input_terms(grads, gate, up, effort):
    tile = 512
    n, (units, width) = grads.shape[1], gate.shape
    m = n // 2

    def kernel(grads_ref, gate_ref, up_ref, own_ref, other_ref, left, right):
        left[...] = grads_ref[...].T
        right[...] = jnp.zeros_like(right)

        @pl.loop(0, width // tile)
        def _(step):
            at = pl.ds(pl.multiple_of(step * tile, tile), tile)
            right[:units, :] = gate_ref[:, at]
            right[GAP : GAP + units, :] = up_ref[:, at]
            term = half(matmul(left[...], right[...]))
            own_ref[:, at] = term[:m]
            other_ref[:, at] = term[m:]

    return pl.pallas_call(
        kernel,
        in_specs=[ON_CHIP] * 3,
        out_specs=[ON_CHIP] * 2,
        out_shape=[jax.ShapeDtypeStruct((m, width), jnp.bfloat16)] * 2,
        scratch_shapes=[
            pltpu.VMEM((n, 2 * GAP), jnp.bfloat16),
            pltpu.VMEM((2 * GAP, tile), jnp.bfloat16),
        ],
        compiler_params=pltpu.CompilerParams(vmem_limit_bytes=TERM << 20),
        cost_estimate=cost(effort),
    )(grads, gate, up)


def weight_grads(pairs, hiddens, grads, first, count, earlier, effort):
    tile = 512
    n = len(pairs)
    units, width = hiddens[0].shape[0], pairs[0].shape[1]
    total = sum(p.shape[0] for p in pairs) // 2
    kept = len(earlier)

    def kernel(*refs):
        pair_refs, hidden_refs, grads_refs = refs[:n], refs[n : n + n // 2], refs[n + n // 2 : 2 * n]
        gate_out, up_out, down_out = refs[2 * n + kept : 2 * n + kept + 3]
        acts, rows_grads, hidden, grad, sems = refs[2 * n + kept + 3 :]
        step = pl.program_id(0)

        def copies(at, slot):
            columns = pl.ds(pl.multiple_of((first + at) * tile, tile), tile)
            made, start = [], 0
            for k in range(n):
                m = pairs[k].shape[0] // 2
                for part, dst in ((0, acts), (1, rows_grads)):
                    made.append(
                        pltpu.make_async_copy(
                            pair_refs[k].at[pl.ds(part * m, m), columns],
                            dst.at[slot, pl.ds(start, m), :],
                            sems.at[slot, 2 * k + part],
                        )
                    )
                start += m
            return made

        @pl.when(step == 0)
        def _():
            for c in copies(0, 0):
                c.start()
            start = 0
            for k in range(n // 2):
                m = hidden_refs[k].shape[1]
                hidden[:, start : start + m] = hidden_refs[k][...]
                grad[:units, start : start + m] = grads_refs[k][:units, :]
                grad[units:, start : start + m] = grads_refs[k][GAP : GAP + units, :]
                start += m

        slot = lax.rem(step, 2)

        @pl.when(step + 1 < count)
        def _():
            for c in copies(step + 1, 1 - slot):
                c.start()

        for c in copies(step, slot):
            c.wait()
        both = half(matmul(grad[...], acts[slot]))
        gate_out[...] = both[:units]
        up_out[...] = both[units:]
        down_out[...] = half(matmul(hidden[...], rows_grads[slot]))

    whole = [
        pl.BlockSpec(v.shape, lambda j: (0, 0), pipeline_mode=pl.Buffered(1)) for v in hiddens + grads
    ]
    hbm = pl.BlockSpec(memory_space=pl.ANY)
    return pl.pallas_call(
        kernel,
        grid=(count,),
        in_specs=[hbm] * n + whole + [hbm] * kept,
        out_specs=[pl.BlockSpec((units, tile), lambda j: (0, first + j))] * 3,
        out_shape=[jax.ShapeDtypeStruct((units, width), jnp.bfloat16)] * 3,
        input_output_aliases={2 * n + i: i for i in range(kept)},
        scratch_shapes=[
            pltpu.VMEM((2, total, tile), jnp.bfloat16),
            pltpu.VMEM((2, total, tile), jnp.bfloat16),
            pltpu.VMEM((units, total), jnp.bfloat16),
            pltpu.VMEM((2 * units, total), jnp.bfloat16),
            pltpu.SemaphoreType.DMA((2, 2 * n)),
        ],
        compiler_params=pltpu.CompilerParams(vmem_limit_bytes=SUMS << 20),
        cost_estimate=cost(effort),
    )(*pairs, *hiddens, *grads, *earlier)


def together(*values):
    return lax.optimization_barrier(values)


def per_device(
    activations, upstream_grad, routes, router_probs, gate_weight, up_weight, down_weight
):
    local_acts = activations[0, 0]
    local_grads = upstream_grad[0, 0]
    expert_hits = routes[0, 0] == 0
    router_weight = jnp.sum(jnp.where(expert_hits, router_probs[0, 0], jnp.float32(0.0)), axis=1)
    is_routed = jnp.any(expert_hits, axis=1)
    before = jnp.arange(256)[None, :] <= jnp.arange(256)[:, None]
    count = jnp.sum(jnp.where(before & is_routed[None, :], 1, 0), axis=1)
    slot = jnp.where(is_routed, count, 0)
    wanted = jnp.arange(1, CAP + 1, dtype=jnp.int32)
    picker = half(slot[None, :] == wanted[:, None])
    scaled = half(router_weight[:, None] * full(local_grads))
    a = half(matmul(picker, local_acts))
    g = half(matmul(picker, scaled))
    gate_local, up_local, down_local = gate_weight[0], up_weight[0], down_weight[0]

    weights = (gate_local, up_local, down_local)

    a, g = together(a, g)
    a_is, a_os, g_sb, g_su = send(a, INNER), send(a, OUTER), send(g, UP), send(g, DOWN)
    to_i, to_o, to_u, to_b, slot_out, a, g = together(
        join(a_os[:32], g, g_sb, g_su),
        join(a_is[32:], g, g_sb, g_su),
        join(g_sb[:32], a, a_is, a_os),
        join(g_su[32:], a, a_is, a_os),
        slot,
        a,
        g,
    )
    from_i, from_o, from_b, from_u = send(to_i, INNER), send(to_o, OUTER), send(to_u, UP), send(to_b, DOWN)
    next_slot = lax.ppermute(slot_out, "section", [(1, 0), (2, 1), (3, 2)])
    own_pair = join(
        a, a_is, from_b[32:160], from_u[32:160],
        g, from_i[32:96], g_sb, from_i[96:160], g_su, from_i[160:224],
    )
    x1_pair = join(a_os, from_b[160:224], from_u[160:224], from_o[32:224])
    a_ts, g_st = join(from_i[:32], from_o[:32]), join(from_b[:32], from_u[:32])
    to_i, to_o, to_u, to_b, own_pair, a_ts, g_st, next_slot = together(
        join(g_st, from_o[32:128]),
        join(g_st, from_i[128:224]),
        join(from_b[32:96], a_ts, from_b[160:192]),
        join(from_u[96:160], a_ts, from_u[192:224]),
        own_pair, a_ts, g_st, next_slot,
    )
    more_i, more_o, more_b, more_u = send(to_i, INNER), send(to_o, OUTER), send(to_u, UP), send(to_b, DOWN)
    own_other = send(own_pair, SIBLING)
    hidden_own, grads_own = forward(own_pair, own_other, *weights, 1 << 20)
    term_own, term_own2 = input_terms(grads_own, gate_local, up_local, 1 << 36)
    term_own, term_own2, more_i, more_o, more_b, more_u = together(
        term_own, term_own2, more_i, more_o, more_b, more_u
    )
    far_pair = join(more_b[:64], more_u[:64], g_st, more_i[:64])
    to_o = join(more_u[:64], more_i[:64])
    far_other = send(far_pair, SIBLING)
    term_from = send(term_own2, SIBLING)
    hidden_far, grads_far = forward(far_pair, far_other, *weights, 1 << 20)
    term_far, term_far2 = input_terms(grads_far, gate_local, up_local, 1 << 36)
    term_far2, term_from = together(term_far2, term_from)
    far_from = send(term_far2, SIBLING)
    own = half(full(term_own) + full(term_from))
    far = half(full(term_far) + full(far_from))
    to_b, to_u, to_i, own0, far0, to_o, more_i, more_o, more_b, more_u, x1_pair = together(
        own[128:256], own[256:384], far[64:128], own[:128], far[:64], to_o,
        more_i, more_o, more_b, more_u, x1_pair,
    )
    z_u, z_b, far_i, tt = send(to_b, DOWN), send(to_u, UP), send(to_i, INNER), send(to_o, OUTER)
    x1_other = send(x1_pair, SIBLING)
    x2_pair = join(
        more_b[64:160], more_u[128:160], more_u[64:128], a_ts,
        more_i[128:160], more_o[64:96], more_o[:64], more_o[96:160], more_i[64:128],
    )
    x2_other = send(x2_pair, SIBLING)
    hidden_x1, grads_x1 = forward(x1_pair, x1_other, *weights, 1 << 36)
    hidden_x2, grads_x2 = forward(x2_pair, x2_other, *weights, 1 << 36)
    z_u, z_b, far_i, hidden_x1, hidden_x2 = together(z_u, z_b, far_i, hidden_x1, hidden_x2)
    near = full(own0) + full(z_u) + full(z_b)
    to_i, to_t, near_s, x3_pair = together(
        half(near[64:]), half(full(far0) + full(far_i)), near[:64], tt
    )
    x3_other = send(x3_pair, SIBLING)
    hidden_x3, grads_x3 = forward(x3_pair, x3_other, *weights, 1 << 36)
    near_i, far_t = send(to_i, INNER), send(to_t, ACROSS)
    pairs = [
        own_pair, own_other, far_pair, far_other,
        x1_pair, x1_other, x2_pair, x2_other, x3_pair, x3_other,
    ]
    hiddens = [hidden_own, hidden_far, hidden_x1, hidden_x2, hidden_x3]
    grads = [grads_own, grads_far, grads_x1, grads_x2, grads_x3]
    early = weight_grads(pairs, hiddens, grads, 0, 4, (), 1 << 36)
    near_i, far_t, near_s, early = together(near_i, far_t, near_s, tuple(early))
    input_rows = half(near_s + full(near_i) + full(far_t))
    shifted = lax.ppermute(input_rows, "section", [(1, 0), (2, 1), (3, 2)])
    placer = half(next_slot[:, None] == wanted[None, :])
    grad_gate, grad_up, grad_down = weight_grads(pairs, hiddens, grads, 4, 4, early, 1 << 36)
    prev_grad = half(matmul(placer, shifted))[None, None]
    return (grad_gate[None], grad_up[None], grad_down[None], prev_grad)


def solution(mesh):
    placed = (
        P("cuts", "section", "dp", None),
        P("cuts", "section", "dp", None),
        P("cuts", "section", "dp", None),
        P("cuts", "section", "dp", None),
        P("section", "dp", None),
        P("section", "dp", None),
        P("section", "dp", None),
    )
    return jax.shard_map(
        per_device,
        mesh=mesh,
        in_specs=placed,
        out_specs=(
            P("section", "dp", None),
            P("section", "dp", None),
            P("section", "dp", None),
            P("cuts", "section", "dp", None),
        ),
        check_vma=False,
    )
```

```python
import jax
import jax.numpy as jnp
from jax import lax
from jax.experimental import pallas as pl
from jax.experimental.pallas import tpu as pltpu
from jax.sharding import PartitionSpec as P

CAP = 64
AXES = ("cuts", "dp")


def place(x, z, core):
    return (x // 2) * 16 + z * 4 + (x % 2) * 2 + core


def route(fx, fz, fc):
    return [
        (place(x, z, c), place(fx(x) % 4, fz(z) % 4, fc(c)))
        for x in range(4)
        for z in range(4)
        for c in range(2)
    ]


def keep(v):
    return v


INNER = route(lambda x: x ^ 1, keep, keep)
OUTER = route(lambda x: 3 - x, keep, keep)
UP = route(keep, lambda z: z + 1, keep)
DOWN = route(keep, lambda z: z - 1, keep)
ACROSS = route(keep, lambda z: z + 2, keep)
SIBLING = route(keep, keep, lambda c: 1 - c)


def send(value, pairs):
    return lax.ppermute(value, AXES, pairs)


def join(*parts):
    return jnp.concatenate(parts, axis=0)


def contract_last(left, right):
    return lax.dot_general(
        left, right, (((1,), (1,)), ((), ())), preferred_element_type=jnp.float32
    )


def contract_first(left, right):
    return lax.dot_general(
        left, right, (((0,), (0,)), ((), ())), preferred_element_type=jnp.float32
    )


def matmul(left, right):
    return jnp.dot(left, right, preferred_element_type=jnp.float32)


def half(v):
    return v.astype(jnp.bfloat16)


def full(v):
    return v.astype(jnp.float32)


GAP = 384
FWD, TERM, SUMS = 14, 10, 44
ON_CHIP = pl.BlockSpec(memory_space=pltpu.VMEM)


def cost(effort):
    return pl.CostEstimate(flops=effort, bytes_accessed=1 << 16, transcendentals=0)


def forward(pair, other, gate, up, down, effort):
    tile = 1024
    m, (units, width) = pair.shape[0] // 2, gate.shape

    def kernel(pair_ref, other_ref, gate_ref, up_ref, down_ref, hidden_ref, grads_ref, acc):
        acc[...] = jnp.zeros_like(acc)

        @pl.loop(0, width // tile)
        def _(step):
            at = pl.ds(pl.multiple_of(step * tile, tile), tile)
            rows_acts = join(pair_ref[:m, at], other_ref[:m, at])
            rows_grads = join(pair_ref[m:, at], other_ref[m:, at])
            acc[0] += contract_last(gate_ref[:, at], rows_acts)
            acc[1] += contract_last(up_ref[:, at], rows_acts)
            acc[2] += contract_last(down_ref[:, at], rows_grads)

        gate_pre, up_pre, hidden_grad = acc[0], acc[1], acc[2]
        sig_gate = jax.nn.sigmoid(gate_pre)
        silu_gate = gate_pre * sig_gate
        hidden_ref[...] = half(silu_gate * up_pre)
        grads_ref[:units, :] = half(
            hidden_grad * up_pre * sig_gate * (1.0 + gate_pre * (1.0 - sig_gate))
        )
        grads_ref[GAP : GAP + units, :] = half(hidden_grad * silu_gate)
        blank = jnp.zeros((GAP - units, 2 * m), jnp.bfloat16)
        grads_ref[units:GAP, :] = blank
        grads_ref[GAP + units :, :] = blank

    return pl.pallas_call(
        kernel,
        in_specs=[ON_CHIP] * 5,
        out_specs=[ON_CHIP] * 2,
        out_shape=[
            jax.ShapeDtypeStruct((units, 2 * m), jnp.bfloat16),
            jax.ShapeDtypeStruct((2 * GAP, 2 * m), jnp.bfloat16),
        ],
        scratch_shapes=[pltpu.VMEM((3, units, 2 * m), jnp.float32)],
        compiler_params=pltpu.CompilerParams(vmem_limit_bytes=FWD << 20),
        cost_estimate=cost(effort),
    )(pair, other, gate, up, down)


def input_terms(grads, gate, up, effort):
    tile = 512
    n, (units, width) = grads.shape[1], gate.shape
    m = n // 2

    def kernel(grads_ref, gate_ref, up_ref, own_ref, other_ref, left, right):
        left[...] = grads_ref[...].T
        right[...] = jnp.zeros_like(right)

        @pl.loop(0, width // tile)
        def _(step):
            at = pl.ds(pl.multiple_of(step * tile, tile), tile)
            right[:units, :] = gate_ref[:, at]
            right[GAP : GAP + units, :] = up_ref[:, at]
            term = half(matmul(left[...], right[...]))
            own_ref[:, at] = term[:m]
            other_ref[:, at] = term[m:]

    return pl.pallas_call(
        kernel,
        in_specs=[ON_CHIP] * 3,
        out_specs=[ON_CHIP] * 2,
        out_shape=[jax.ShapeDtypeStruct((m, width), jnp.bfloat16)] * 2,
        scratch_shapes=[
            pltpu.VMEM((n, 2 * GAP), jnp.bfloat16),
            pltpu.VMEM((2 * GAP, tile), jnp.bfloat16),
        ],
        compiler_params=pltpu.CompilerParams(vmem_limit_bytes=TERM << 20),
        cost_estimate=cost(effort),
    )(grads, gate, up)


def weight_grads(pairs, hiddens, grads, first, count, earlier, effort):
    tile = 512
    n = len(pairs)
    units, width = hiddens[0].shape[0], pairs[0].shape[1]
    total = sum(p.shape[0] for p in pairs) // 2
    kept = len(earlier)

    def kernel(*refs):
        pair_refs, hidden_refs, grads_refs = refs[:n], refs[n : n + n // 2], refs[n + n // 2 : 2 * n]
        gate_out, up_out, down_out = refs[2 * n + kept : 2 * n + kept + 3]
        acts, rows_grads, hidden, grad, sems = refs[2 * n + kept + 3 :]
        step = pl.program_id(0)

        def copies(at, slot):
            columns = pl.ds(pl.multiple_of((first + at) * tile, tile), tile)
            made, start = [], 0
            for k in range(n):
                m = pairs[k].shape[0] // 2
                for part, dst in ((0, acts), (1, rows_grads)):
                    made.append(
                        pltpu.make_async_copy(
                            pair_refs[k].at[pl.ds(part * m, m), columns],
                            dst.at[slot, pl.ds(start, m), :],
                            sems.at[slot, 2 * k + part],
                        )
                    )
                start += m
            return made

        @pl.when(step == 0)
        def _():
            for c in copies(0, 0):
                c.start()
            start = 0
            for k in range(n // 2):
                m = hidden_refs[k].shape[1]
                hidden[:, start : start + m] = hidden_refs[k][...]
                grad[:units, start : start + m] = grads_refs[k][:units, :]
                grad[units:, start : start + m] = grads_refs[k][GAP : GAP + units, :]
                start += m

        slot = lax.rem(step, 2)

        @pl.when(step + 1 < count)
        def _():
            for c in copies(step + 1, 1 - slot):
                c.start()

        for c in copies(step, slot):
            c.wait()
        both = half(matmul(grad[...], acts[slot]))
        gate_out[...] = both[:units]
        up_out[...] = both[units:]
        down_out[...] = half(matmul(hidden[...], rows_grads[slot]))

    whole = [ON_CHIP] * len(hiddens + grads)
    hbm = pl.BlockSpec(memory_space=pl.ANY)
    return pl.pallas_call(
        kernel,
        grid=(count,),
        in_specs=[hbm] * n + whole + [hbm] * kept,
        out_specs=[pl.BlockSpec((units, tile), lambda j: (0, first + j))] * 3,
        out_shape=[jax.ShapeDtypeStruct((units, width), jnp.bfloat16)] * 3,
        input_output_aliases={2 * n + i: i for i in range(kept)},
        scratch_shapes=[
            pltpu.VMEM((2, total, tile), jnp.bfloat16),
            pltpu.VMEM((2, total, tile), jnp.bfloat16),
            pltpu.VMEM((units, total), jnp.bfloat16),
            pltpu.VMEM((2 * units, total), jnp.bfloat16),
            pltpu.SemaphoreType.DMA((2, 2 * n)),
        ],
        compiler_params=pltpu.CompilerParams(vmem_limit_bytes=SUMS << 20),
        cost_estimate=cost(effort),
    )(*pairs, *hiddens, *grads, *earlier)


def together(*values):
    return lax.optimization_barrier(values)


def per_device(
    activations, upstream_grad, routes, router_probs, gate_weight, up_weight, down_weight
):
    local_acts = activations[0, 0]
    local_grads = upstream_grad[0, 0]
    expert_hits = routes[0, 0] == 0
    router_weight = jnp.sum(jnp.where(expert_hits, router_probs[0, 0], jnp.float32(0.0)), axis=1)
    is_routed = jnp.any(expert_hits, axis=1)
    before = jnp.arange(256)[None, :] <= jnp.arange(256)[:, None]
    count = jnp.sum(jnp.where(before & is_routed[None, :], 1, 0), axis=1)
    slot = jnp.where(is_routed, count, 0)
    wanted = jnp.arange(1, CAP + 1, dtype=jnp.int32)
    picker = half(slot[None, :] == wanted[:, None])
    scaled = half(router_weight[:, None] * full(local_grads))
    a = half(matmul(picker, local_acts))
    g = half(matmul(picker, scaled))
    gate_local, up_local, down_local = gate_weight[0], up_weight[0], down_weight[0]

    weights = (gate_local, up_local, down_local)

    a, g = together(a, g)
    a_is, a_os, g_sb, g_su = send(a, INNER), send(a, OUTER), send(g, UP), send(g, DOWN)
    to_i, to_o, to_u, to_b, slot_out, a, g = together(
        join(a_os[:32], g, g_sb, g_su),
        join(a_is[32:], g, g_sb, g_su),
        join(g_sb[:32], a, a_is, a_os),
        join(g_su[32:], a, a_is, a_os),
        slot,
        a,
        g,
    )
    from_i, from_o, from_b, from_u = send(to_i, INNER), send(to_o, OUTER), send(to_u, UP), send(to_b, DOWN)
    next_slot = lax.ppermute(slot_out, "section", [(1, 0), (2, 1), (3, 2)])
    own_pair = join(
        a, a_is, from_b[32:160], from_u[32:160],
        g, from_i[32:96], g_sb, from_i[96:160], g_su, from_i[160:224],
    )
    x1_pair = join(a_os, from_b[160:224], from_u[160:224], from_o[32:224])
    a_ts, g_st = join(from_i[:32], from_o[:32]), join(from_b[:32], from_u[:32])
    to_i, to_o, to_u, to_b, own_pair, a_ts, g_st, next_slot = together(
        join(g_st, from_o[32:128]),
        join(g_st, from_i[128:224]),
        join(from_b[32:96], a_ts, from_b[160:192]),
        join(from_u[96:160], a_ts, from_u[192:224]),
        own_pair, a_ts, g_st, next_slot,
    )
    more_i, more_o, more_b, more_u = send(to_i, INNER), send(to_o, OUTER), send(to_u, UP), send(to_b, DOWN)
    own_other = send(own_pair, SIBLING)
    hidden_own, grads_own = forward(own_pair, own_other, *weights, 1 << 20)
    term_own, term_own2 = input_terms(grads_own, gate_local, up_local, 1 << 20)
    term_own, term_own2, more_i, more_o, more_b, more_u = together(
        term_own, term_own2, more_i, more_o, more_b, more_u
    )
    a_tt, g_tt = send(more_u[:64], OUTER), send(more_o[:64], INNER)
    far_pair = join(more_b[:64], more_u[:64], g_st, more_i[:64])
    far_other = send(far_pair, SIBLING)
    term_from = send(term_own2, SIBLING)
    hidden_far, grads_far = forward(far_pair, far_other, *weights, 1 << 36)
    term_far, term_far2 = input_terms(grads_far, gate_local, up_local, 1 << 20)
    term_far2, term_from = together(term_far2, term_from)
    far_from = send(term_far2, SIBLING)
    own = half(full(term_own) + full(term_from))
    far = half(full(term_far) + full(far_from))
    to_b, to_u, to_i, own0, far0, a_tt, g_tt, more_i, more_o, more_b, more_u, x1_pair = together(
        own[128:256], own[256:384], far[64:128], own[:128], far[:64], a_tt, g_tt,
        more_i, more_o, more_b, more_u, x1_pair,
    )
    z_u, z_b, far_i = send(to_b, DOWN), send(to_u, UP), send(to_i, INNER)
    x1_other = send(x1_pair, SIBLING)
    x1_other, more_b, more_u, a_tt = together(x1_other, more_b, more_u, a_tt)
    x2_pair = join(
        more_b[64:160], more_u[128:160], more_u[64:128], a_ts, a_tt,
        more_i[128:160], more_o[64:96], more_o[:64], more_o[96:160], more_i[64:128], g_tt,
    )
    x2_other = send(x2_pair, SIBLING)
    hidden_x1, grads_x1 = forward(x1_pair, x1_other, *weights, 1 << 36)
    hidden_x2, grads_x2 = forward(x2_pair, x2_other, *weights, 1 << 36)
    z_u, z_b, far_i, hidden_x1, hidden_x2 = together(z_u, z_b, far_i, hidden_x1, hidden_x2)
    near = full(own0) + full(z_u) + full(z_b)
    to_i, to_t, near_s = together(half(near[64:]), half(full(far0) + full(far_i)), near[:64])
    near_i, far_t = send(to_i, INNER), send(to_t, ACROSS)
    pairs = [
        own_pair, own_other, far_pair, far_other,
        x1_pair, x1_other, x2_pair, x2_other,
    ]
    hiddens = [hidden_own, hidden_far, hidden_x1, hidden_x2]
    grads = [grads_own, grads_far, grads_x1, grads_x2]
    early = weight_grads(pairs, hiddens, grads, 0, 4, (), 1 << 36)
    near_i, far_t, near_s, early = together(near_i, far_t, near_s, tuple(early))
    input_rows = half(near_s + full(near_i) + full(far_t))
    shifted = lax.ppermute(input_rows, "section", [(1, 0), (2, 1), (3, 2)])
    placer = half(next_slot[:, None] == wanted[None, :])
    grad_gate, grad_up, grad_down = weight_grads(pairs, hiddens, grads, 4, 4, early, 1 << 36)
    prev_grad = half(matmul(placer, shifted))[None, None]
    return (grad_gate[None], grad_up[None], grad_down[None], prev_grad)


def solution(mesh):
    placed = (
        P("cuts", "section", "dp", None),
        P("cuts", "section", "dp", None),
        P("cuts", "section", "dp", None),
        P("cuts", "section", "dp", None),
        P("section", "dp", None),
        P("section", "dp", None),
        P("section", "dp", None),
    )
    return jax.shard_map(
        per_device,
        mesh=mesh,
        in_specs=placed,
        out_specs=(
            P("section", "dp", None),
            P("section", "dp", None),
            P("section", "dp", None),
            P("cuts", "section", "dp", None),
        ),
        check_vma=False,
    )
```
